32 devices in a mesh: scen: 16 (over z, y, x), net: 2 (over core).
Axes of the slice: x: 2, y: 2, z: 4, core: 2. Of those that a mesh axis runs over, the one named last changes fastest.
Arguments:
- prior_mean: float32 [64, 32, 128], P('scen', 'net'), may hold values from 0 to 2
- multipliers: float32 [64, 32, 128], P('scen', 'net'), may hold values from -4 to 4
- demand: float32 [64, 32, 128], P('scen', 'net'), may hold values from -6 to 6
- linear_cost: float32 [32, 128], P('net'), may hold values from -4 to 4
- penalty: float32 [32, 128], P('net'), may hold values from 0.5 to 4
- constraint_blocks: float32 [32, 4, 128, 128], P('net'), may hold values from -0.25 to 0.25
- block_columns: int32 [32, 4], P('net'), may hold values from 0 to 19, as said below
- block_section: int32 [32], P('net'), may hold values from 0 to 5
Outputs:
- consensus: float32 [64, 32, 128], P('scen', 'net')
- new_multipliers: float32 [64, 32, 128], P('scen', 'net')
The draws below stay inside these ranges and needn't reach their ends.
Inputs may be any that keep to these rules, and one draw needn't show every extreme that they name: block_columns[i, 0] is 2 plus the position of block i among its partition's 16 blocks; every other entry differs from it by 1 to 2 blocks; in each partition the first block reaches 2 blocks before it and the last one 2 blocks after it.
All inputs are finite; a program needn't handle non-finite values.
Results may differ from the reference program's by a relative error of at most 0.00015.
Values sent between devices are 32-bit elements; how exact they have to be, the bound alone decides.
A program may use at most 64 MiB of HBM per device.

```python
import math
import jax
import jax.numpy as jnp
from jax import lax

BLK = 128
NNZ = 4
HB = 2
SECTIONS = 6
ITERS = 2
NB_DEV = 16
SCEN = 64
NBLK = 32


def draw_block_columns(key, part):
    position = jnp.arange(NBLK, dtype=jnp.int32) % NB_DEV
    raw_picks = jax.random.randint(key, (NBLK, NNZ - 1), 0, 2 * HB)
    offsets = jnp.where(raw_picks < HB, raw_picks - HB, raw_picks - HB + 1)
    first_offset = jnp.where(position == 0, -HB, jnp.where(position == NB_DEV - 1, HB, offsets[:, 0]))
    offsets = jnp.concatenate([first_offset[:, None], offsets[:, 1:]], axis=1)
    centre = (position + HB)[:, None]
    return jnp.concatenate([centre, centre + offsets], axis=1).astype(jnp.int32)


def plant(array, own_key, low, top_value):
    dims = array.shape
    index_at = [jax.random.randint(jax.random.fold_in(own_key, axis), (), 0, dims[axis]) for axis in range(len(dims))]
    array = array.at[tuple(index_at)].set(low)
    longest = dims.index(max(dims))
    index_at[longest] = (index_at[longest] + 1) % dims[longest]
    return array.at[tuple(index_at)].set(top_value)


def block_scale(own_key, dims, shards, low, largest):
    def one(axis_at, shards_of):
        heights = jax.random.uniform(jax.random.fold_in(jax.random.fold_in(own_key, 6), axis_at), (shards_of,), jnp.float32, low / len(shards), largest / len(shards))
        return jnp.repeat(jnp.exp(heights), dims[axis_at] // shards_of).reshape((-1,) + (1,) * (len(dims) - axis_at - 1))

    loudness = one(*shards[0])
    for cut in shards[1:]:
        loudness = loudness * one(*cut)
    return loudness


def centred(stream_key, shape, scale, most, cuts=(), kind=jnp.bfloat16):
    loudness = block_scale(stream_key, shape, cuts, -0.22, 0.18) if cuts else 1.0
    entries = jax.random.normal(stream_key, shape, jnp.float32) * scale * loudness
    return jnp.minimum(jnp.maximum(entries, -most), most).astype(kind)


def setup_inputs(seed: int = 0) -> dict:
    key_list = jax.random.split(jax.random.key(seed), 9)
    return {
        "prior_mean": jnp.clip(2.0 * jax.random.uniform(key_list[0], (SCEN, NBLK, BLK), jnp.float32) ** block_scale(key_list[0], (SCEN, NBLK, BLK), ((0, 16), (1, 2)), -0.2, 0.2), 0.0, 2.0),
        "multipliers": centred(key_list[1], (SCEN, NBLK, BLK), 0.5, 4.0, ((0, 16), (1, 2)), jnp.float32),
        "demand": centred(key_list[2], (SCEN, NBLK, BLK), 1.0, 6.0, ((0, 16), (1, 2)), jnp.float32),
        "linear_cost": centred(key_list[3], (NBLK, BLK), 0.5, 4.0, ((0, 2),), jnp.float32),
        "penalty": jnp.clip(jnp.exp(math.log(4.0) - 2.0794415 * jax.random.uniform(key_list[4], (NBLK, BLK), jnp.float32) ** block_scale(key_list[4], (NBLK, BLK), ((0, 2),), -0.2, 0.2)), 0.5, 4.0),
        "constraint_blocks": centred(key_list[5], (NBLK, NNZ, BLK, BLK), (NNZ * BLK) ** -0.5, 0.25, ((0, 2),), jnp.float32),
        "block_columns": draw_block_columns(jax.random.fold_in(key_list[8], 71), 0),
        "block_section": plant(jax.random.randint(key_list[7], (NBLK,), 0, SECTIONS), jax.random.fold_in(key_list[7], 1), 0, SECTIONS - 1).astype(jnp.int32),
    }


exact_mode = lax.Precision.HIGHEST


def global_columns(block_columns):
    base_block = (jnp.arange(NBLK, dtype=jnp.int32) // NB_DEV) * NB_DEV
    return base_block[:, None] + block_columns.astype(jnp.int32)


def apply_forward(constraint_blocks, columns, values):
    padded = jnp.pad(values, ((0, 0), (HB, HB), (0, 0)))
    picked = padded[:, columns]
    return jnp.einsum("ikrc,sikc->sir", constraint_blocks, picked, precision=exact_mode)


def apply_transpose(constraint_blocks, columns, values):
    block_terms = jnp.einsum("ikrc,sir->sikc", constraint_blocks, values, precision=exact_mode)
    padded = jnp.zeros((values.shape[0], NBLK + 2 * HB, BLK), dtype=jnp.float32)
    padded = padded.at[:, columns].add(block_terms)
    return padded[:, HB:HB + NBLK]


def reference(prior_mean, multipliers, demand, linear_cost, penalty, constraint_blocks, block_columns, block_section):
    columns = global_columns(block_columns)
    residual = apply_transpose(constraint_blocks, columns, demand - apply_forward(constraint_blocks, columns, prior_mean))
    residual = residual - linear_cost[None] - multipliers
    primal = prior_mean
    direction = residual
    norm_now = jnp.sum(residual * residual, axis=(1, 2))
    for sweep in range(ITERS):
        curved = penalty[None] * direction + apply_transpose(constraint_blocks, columns, apply_forward(constraint_blocks, columns, direction))
        step_size = norm_now / jnp.sum(direction * curved, axis=(1, 2))
        primal = primal + step_size[:, None, None] * direction
        residual = residual - step_size[:, None, None] * curved
        norm_next = jnp.sum(residual * residual, axis=(1, 2))
        direction = residual + (norm_next / norm_now)[:, None, None] * direction
        norm_now = norm_next
    clipped = jnp.maximum(primal, 0.0)
    consensus = jnp.zeros_like(clipped)
    for section in range(SECTIONS):
        group_size = SCEN >> section
        grouped = clipped.reshape(SCEN // group_size, group_size, NBLK, BLK)
        averaged = jnp.sum(grouped, axis=1, keepdims=True) / group_size
        averaged = jnp.broadcast_to(averaged, grouped.shape).reshape(clipped.shape)
        consensus = jnp.where((block_section == section)[None, :, None], averaged, consensus)
    new_multipliers = multipliers + penalty[None] * (clipped - consensus)
    return consensus, new_multipliers
```

```python
import functools

import jax
import jax.numpy as jnp
from jax import lax
from jax.experimental import pallas as pl
from jax.experimental.pallas import tpu as pltpu
from jax.sharding import PartitionSpec as P

HB = 2
MESH = pl.DeviceIdType.MESH


def phases_of(nodes):
    bits = nodes.bit_length() - 1
    out = []
    at = 0
    while at < bits:
        take = min(2, bits - at)
        out.append((at, [m << at for m in range(1, 1 << take)]))
        at += take
    return out


def kernel(
    nets,
    nodes,
    x_hbm,
    lam_hbm,
    dem_hbm,
    cost_hbm,
    pen_hbm,
    mat_hbm,
    col_hbm,
    sec_hbm,
    cons_ref,
    newm_ref,
    x_in,
    lam_in,
    dem_in,
    cost_in,
    pen_in,
    mat_in,
    cols,
    secs,
    split,
    xv,
    bv,
    dv,
    penb,
    hl,
    rv,
    w0,
    sec_rows,
    x_got,
    msg_out,
    msg_in,
    sum_out,
    sum_in,
    in_sem,
    mat_sem,
    xs_sem,
    xr_sem,
    ms_sem,
    mr_sem,
    ss_sem,
    sr_sem,
):
    L, nb, blk = x_in.shape
    nnz = mat_in.shape[1]
    R = 2 * L
    me_s = lax.axis_index("scen")
    me_n = lax.axis_index("net")
    phases = phases_of(nodes)

    small = [
        pltpu.make_async_copy(src, dst, in_sem.at[j])
        for j, (src, dst) in enumerate(
            [
                (x_hbm, x_in),
                (col_hbm, cols),
                (dem_hbm, dem_in),
                (lam_hbm, lam_in),
                (cost_hbm, cost_in),
                (pen_hbm, pen_in),
                (sec_hbm, secs),
            ]
        )
    ]
    for copy in small:
        copy.start()
    mats = [pltpu.make_async_copy(mat_hbm.at[i], mat_in.at[i], mat_sem.at[i]) for i in range(nb)]
    for copy in mats:
        copy.start()

    net_peer = [lax.rem(me_n + p, nets) for p in range(1, nets)]
    barrier = pltpu.get_barrier_semaphore()
    count = 0
    for peer in net_peer:
        pl.semaphore_signal(barrier, inc=1, device_id=(me_s, peer), device_id_type=MESH)
        count += 1

    def scen_peer(at, mask):
        bit = mask >> at
        low = lax.rem(me_s // (1 << at), 2)
        flipped = me_s
        if bit & 1:
            flipped = flipped + (1 - 2 * low) * (1 << at)
        if bit & 2:
            high = lax.rem(me_s // (2 << at), 2)
            flipped = flipped + (1 - 2 * high) * (2 << at)
        return flipped

    for at, masks in phases:
        for mask in masks:
            pl.semaphore_signal(
                barrier, inc=1, device_id=(scen_peer(at, mask), me_n), device_id_type=MESH
            )
            count += 1

    has_left = me_n > 0
    has_right = me_n < nets - 1

    def make_split(i):
        for k in range(nnz):
            a = mat_in[i, k]
            hi = a.astype(jnp.bfloat16)
            split[i, 0:blk, k * blk : (k + 1) * blk] = hi
            split[i, blk : 2 * blk, k * blk : (k + 1) * blk] = (
                a - hi.astype(jnp.float32)
            ).astype(jnp.bfloat16)

    first_half = nb // 2

    @pl.loop(0, first_half)
    def _(i):
        pltpu.make_async_copy(mat_hbm.at[i], mat_in.at[i], mat_sem.at[i]).wait()
        make_split(i)

    pl.semaphore_wait(barrier, count)
    x_sends = [
        pltpu.make_async_remote_copy(
            src_ref=x_hbm,
            dst_ref=x_got.at[p],
            send_sem=xs_sem.at[p],
            recv_sem=xr_sem.at[p],
            device_id=(me_s, peer),
            device_id_type=MESH,
        )
        for p, peer in enumerate(net_peer)
    ]
    for copy in x_sends:
        copy.start()
    for copy in small:
        copy.wait()

    upper = lax.broadcasted_iota(jnp.int32, (R, blk), 0) < L

    def halves(v):
        hi = v.astype(jnp.bfloat16).astype(jnp.float32)
        return jnp.where(upper, hi, v - hi)

    for s in range(L):
        for r in (s, s + L):
            xv[pl.ds(r, nb, stride=R), :] = x_in[s]
            bv[pl.ds(r, nb, stride=R), :] = dem_in[s]
            dv[pl.ds(r, nb, stride=R), :] = cost_in[...] + lam_in[s]
            penb[pl.ds(r, nb, stride=R), :] = pen_in[...]
    for i in range(nb):
        sec_rows[i : i + 1, :] = jnp.full((1, blk), secs[i], jnp.int32)
        hl[HB + i] = halves(xv[i * R : (i + 1) * R, :])

    @pl.loop(first_half, nb)
    def _(i):
        pltpu.make_async_copy(mat_hbm.at[i], mat_in.at[i], mat_sem.at[i]).wait()
        make_split(i)

    for copy in x_sends:
        copy.wait()

    def halo_of_rows(ref, rows):
        return [
            jnp.concatenate([ref[s, r : r + 1] for s in list(range(L)) * 2], axis=0) for r in rows
        ]

    zero = jnp.zeros((R, blk), jnp.float32)

    def set_halo(low, high):
        for j in range(HB):
            hl[j] = halves(jnp.where(has_left, low[j], zero))
            hl[HB + nb + j] = halves(jnp.where(has_right, high[j], zero))

    if nets > 1:
        set_halo(
            halo_of_rows(x_got.at[0], range(nb - HB, nb)),
            halo_of_rows(x_got.at[nets - 2], range(HB)),
        )
    else:
        set_halo([zero] * HB, [zero] * HB)

    def forward_row(i):
        lhs = jnp.concatenate([hl[cols[i, k]] for k in range(nnz)], axis=1).astype(jnp.bfloat16)
        out = lax.dot_general(
            lhs, split[i], (((1,), (1,)), ((), ())), preferred_element_type=jnp.float32
        )
        both = out[:, :blk] + out[:, blk:]
        return both + pltpu.roll(both, L, 0)

    def transpose_row(i, w, acc):
        h = halves(w)
        lhs = jnp.concatenate([h, h], axis=1).astype(jnp.bfloat16)
        out = lax.dot_general(
            lhs, split[i], (((1,), (0,)), ((), ())), preferred_element_type=jnp.float32
        )
        both = out + pltpu.roll(out, L, 0)

        def put(at, term):
            acc[at] = term if acc[at] is None else acc[at] + term

        put(HB + i, both[:, :blk])
        for k in range(1, nnz):
            term = both[:, k * blk : (k + 1) * blk]
            for o in range(-HB, HB + 1):
                if o != 0:
                    put(HB + i + o, jnp.where(cols[i, k] == HB + i + o, term, zero))

    edge = list(range(HB)) + list(range(nb - HB, nb))
    inner = list(range(HB, nb - HB))

    def send(e, blocks, partial):
        for j, b in enumerate(blocks):
            if b is not None:
                msg_out[e, j] = b
        if partial is not None:
            msg_out[e, 2 * HB] = partial
        first = 0 if blocks else 2 * HB
        last = 2 * HB + (1 if partial is not None else 0)
        copies = [
            pltpu.make_async_remote_copy(
                src_ref=msg_out.at[e, pl.ds(first, last - first)],
                dst_ref=msg_in.at[e, p, pl.ds(first, last - first)],
                send_sem=ms_sem.at[e, p],
                recv_sem=mr_sem.at[e, p],
                device_id=(me_s, peer),
                device_id_type=MESH,
            )
            for p, peer in enumerate(net_peer)
        ]
        for copy in copies:
            copy.start()
        return copies

    def neighbours(e):
        if nets == 1:
            return [zero] * HB, [zero] * HB
        low = [jnp.where(has_left, msg_in[e, 0, HB + j], zero) for j in range(HB)]
        high = [jnp.where(has_right, msg_in[e, nets - 2, j], zero) for j in range(HB)]
        return low, high

    def total(e, partial):
        for p in range(nets - 1):
            partial = partial + msg_in[e, p, 2 * HB]
        return jnp.sum(partial, axis=1, keepdims=True)

    def wait(copies):
        for copy in copies:
            copy.wait()

    def transposed(e, w, partial):
        acc = [None] * (nb + 2 * HB)
        for i in edge:
            transpose_row(i, w[i], acc)
        copies = send(e, acc[:HB] + acc[HB + nb :], partial)
        for i in inner:
            transpose_row(i, w[i], acc)
        wait(copies)
        low, high = neighbours(e)
        z = acc[HB : HB + nb]
        for j in range(HB):
            z[j] = z[j] + low[j]
            z[nb - HB + j] = z[nb - HB + j] + high[j]
        return z

    def forward_with_halo(e, v, partial):
        copies = send(e, v[:HB] + v[nb - HB :], partial)
        for i in range(nb):
            hl[HB + i] = halves(v[i])
        w = [None] * nb
        for i in inner:
            w[i] = forward_row(i)
        wait(copies)
        low, high = neighbours(e)
        set_halo(low, high)
        for i in edge:
            w[i] = forward_row(i)
        return w

    def rows(ref):
        return [ref[i * R : (i + 1) * R, :] for i in range(nb)]

    def add_all(terms):
        while len(terms) > 1:
            terms = [
                terms[j] + terms[j + 1] if j + 1 < len(terms) else terms[j]
                for j in range(0, len(terms), 2)
            ]
        return terms[0]

    w = [bv[i * R : (i + 1) * R, :] - forward_row(i) for i in range(nb)]
    z = transposed(0, w, None)
    r0 = [z[i] - dv[i * R : (i + 1) * R, :] for i in range(nb)]
    part0 = add_all([v * v for v in r0])
    for i in range(nb):
        rv[i * R : (i + 1) * R, :] = r0[i]
    wa = forward_with_halo(1, r0, part0)
    norm0 = total(1, part0)
    for i in range(nb):
        w0[i * R : (i + 1) * R, :] = wa[i]
    pen = rows(penb)
    part_q = add_all(
        [p * v * v for p, v in zip(pen, rows(rv))] + [v * v for v in wa]
    )
    z = transposed(2, wa, part_q)
    a0 = norm0 / total(2, part_q)
    r0 = rows(rv)
    pen = rows(penb)
    r1 = [r0[i] - a0 * (pen[i] * r0[i] + z[i]) for i in range(nb)]
    part1 = add_all([v * v for v in r1])
    for i in range(nb):
        dv[i * R : (i + 1) * R, :] = r1[i]
        bv[i * R : (i + 1) * R, :] = xv[i * R : (i + 1) * R, :] + a0 * r0[i]
    wb = forward_with_halo(3, r1, part1)
    norm1 = total(3, part1)
    beta = norm1 / norm0
    d1 = [dv[i * R : (i + 1) * R, :] + beta * rv[i * R : (i + 1) * R, :] for i in range(nb)]
    ad = [wb[i] + beta * w0[i * R : (i + 1) * R, :] for i in range(nb)]
    part_q = add_all(
        [penb[i * R : (i + 1) * R, :] * d1[i] * d1[i] for i in range(nb)] + [v * v for v in ad]
    )
    wait(send(4, [], part_q))
    a1 = norm1 / total(4, part_q)
    for i in range(nb):
        rows_i = slice(i * R, (i + 1) * R)
        xv[rows_i, :] = jnp.maximum(bv[rows_i, :] + a1 * d1[i], 0.0)

    clipped = [xv[pl.ds(s, nb, stride=R), :] for s in range(L)]
    group = jnp.right_shift(jnp.int32(L * nodes), sec_rows[...])
    sums = clipped
    for b in range(L.bit_length() - 1):
        sums = [
            sums[s] + jnp.where(group > (1 << b), sums[s ^ (1 << b)], 0.0) for s in range(L)
        ]
    mine = sums[0]
    base = mine
    slot = 0
    for f, (at, masks) in enumerate(phases):
        sum_out[f] = mine
        copies = []
        for j, mask in enumerate(masks):
            copies.append(
                pltpu.make_async_remote_copy(
                    src_ref=sum_out.at[f],
                    dst_ref=sum_in.at[slot + j],
                    send_sem=ss_sem.at[slot + j],
                    recv_sem=sr_sem.at[slot + j],
                    device_id=(scen_peer(at, mask), me_n),
                    device_id_type=MESH,
                )
            )
        for copy in copies:
            copy.start()
        wait(copies)
        got = [sum_in[slot + j] for j in range(len(masks))]
        extra = jnp.where(group > (L << at), got[0], 0.0)
        if len(masks) == 3:
            extra = extra + jnp.where(group > (L << (at + 1)), got[1] + got[2], 0.0)
        mine = mine + extra
        slot += len(masks)
    shared = group >= L
    size = group.astype(jnp.float32)
    for s in range(L):
        mean = jnp.where(shared, mine, sums[s]) / size
        cons_ref[s] = mean
        newm_ref[s] = lam_in[s] + pen_in[...] * (clipped[s] - mean)


def body(*args):
    x = args[0]
    mat = args[5]
    L, nb, blk = x.shape
    nnz = mat.shape[1]
    nets = lax.axis_size("net")
    nodes = lax.axis_size("scen")
    R = 2 * L
    others = max(nets - 1, 1)
    phases = phases_of(nodes)
    slots = max(sum(len(m) for _, m in phases), 1)
    f32 = jnp.float32
    V = pltpu.VMEM
    dma = pltpu.SemaphoreType.DMA
    scratch = [
        V((L, nb, blk), f32),
        V((L, nb, blk), f32),
        V((L, nb, blk), f32),
        V((nb, blk), f32),
        V((nb, blk), f32),
        V(mat.shape, f32),
        pltpu.SMEM((nb, nnz), jnp.int32),
        pltpu.SMEM((nb,), jnp.int32),
        V((nb, 2 * blk, nnz * blk), jnp.bfloat16),
        V((nb * R, blk), f32),
        V((nb * R, blk), f32),
        V((nb * R, blk), f32),
        V((nb * R, blk), f32),
        V((nb + 2 * HB, R, blk), f32),
        V((nb * R, blk), f32),
        V((nb * R, blk), f32),
        V((nb, blk), jnp.int32),
        V((others, L, nb, blk), f32),
        V((5, 2 * HB + 1, R, blk), f32),
        V((5, others, 2 * HB + 1, R, blk), f32),
        V((max(len(phases), 1), nb, blk), f32),
        V((slots, nb, blk), f32),
        dma((7,)),
        dma((nb,)),
        dma((others,)),
        dma((others,)),
        dma((5, others)),
        dma((5, others)),
        dma((slots,)),
        dma((slots,)),
    ]
    any_spec = pl.BlockSpec(memory_space=pl.ANY)
    vmem_spec = pl.BlockSpec(memory_space=pltpu.VMEM)
    return pl.pallas_call(
        functools.partial(kernel, nets, nodes),
        out_shape=(jax.ShapeDtypeStruct(x.shape, f32), jax.ShapeDtypeStruct(x.shape, f32)),
        in_specs=[any_spec] * 8,
        out_specs=(vmem_spec, vmem_spec),
        scratch_shapes=scratch,
        compiler_params=pltpu.CompilerParams(
            collective_id=0, has_side_effects=True, vmem_limit_bytes=40 << 20
        ),
    )(*args)


def solution(mesh):
    placed = (
        P("scen", "net", None),
        P("scen", "net", None),
        P("scen", "net", None),
        P("net", None),
        P("net", None),
        P("net", None, None, None),
        P("net", None),
        P("net"),
    )
    fn = jax.shard_map(
        body,
        mesh=mesh,
        in_specs=placed,
        out_specs=(P("scen", "net", None), P("scen", "net", None)),
        check_vma=False,
    )
    return lambda *args: tuple(fn(*args))
```

```python
import functools

import jax
import jax.numpy as jnp
from jax import lax
from jax.experimental import pallas as pl
from jax.experimental.pallas import tpu as pltpu
from jax.sharding import PartitionSpec as P

HB = 2
MESH = pl.DeviceIdType.MESH


def phases_of(nodes):
    bits = nodes.bit_length() - 1
    out = []
    at = 0
    while at < bits:
        take = min(2, bits - at)
        out.append((at, [m << at for m in range(1, 1 << take)]))
        at += take
    return out


def kernel(
    nets,
    nodes,
    x_hbm,
    lam_hbm,
    dem_hbm,
    cost_hbm,
    pen_hbm,
    mat_hbm,
    col_hbm,
    sec_hbm,
    cons_ref,
    newm_ref,
    x_in,
    lam_in,
    dem_in,
    cost_in,
    pen_in,
    mat_in,
    cols,
    secs,
    split,
    xv,
    bv,
    dv,
    penb,
    hl,
    rv,
    w0,
    sec_rows,
    x_got,
    msg_out,
    msg_in,
    sum_out,
    sum_in,
    in_sem,
    mat_sem,
    xs_sem,
    xr_sem,
    ms_sem,
    mr_sem,
    ss_sem,
    sr_sem,
):
    L, nb, blk = x_in.shape
    nnz = mat_in.shape[1]
    R = 2 * L
    me_s = lax.axis_index("scen")
    me_n = lax.axis_index("net")
    phases = phases_of(nodes)

    small = [
        pltpu.make_async_copy(src, dst, in_sem.at[j])
        for j, (src, dst) in enumerate(
            [
                (x_hbm, x_in),
                (col_hbm, cols),
                (dem_hbm, dem_in),
                (lam_hbm, lam_in),
                (cost_hbm, cost_in),
                (pen_hbm, pen_in),
                (sec_hbm, secs),
            ]
        )
    ]
    for copy in small:
        copy.start()
    mats = [pltpu.make_async_copy(mat_hbm.at[i], mat_in.at[i], mat_sem.at[i]) for i in range(nb)]
    for copy in mats:
        copy.start()

    net_peer = [lax.rem(me_n + p, nets) for p in range(1, nets)]
    barrier = pltpu.get_barrier_semaphore()
    count = 0
    for peer in net_peer:
        pl.semaphore_signal(barrier, inc=1, device_id=(me_s, peer), device_id_type=MESH)
        count += 1

    def scen_peer(at, mask):
        bit = mask >> at
        low = lax.rem(me_s // (1 << at), 2)
        flipped = me_s
        if bit & 1:
            flipped = flipped + (1 - 2 * low) * (1 << at)
        if bit & 2:
            high = lax.rem(me_s // (2 << at), 2)
            flipped = flipped + (1 - 2 * high) * (2 << at)
        return flipped

    for at, masks in phases:
        for mask in masks:
            pl.semaphore_signal(
                barrier, inc=1, device_id=(scen_peer(at, mask), me_n), device_id_type=MESH
            )
            count += 1

    has_left = me_n > 0
    has_right = me_n < nets - 1

    def make_split(i):
        for k in range(nnz):
            a = mat_in[i, k]
            hi = a.astype(jnp.bfloat16)
            split[i, 0:blk, k * blk : (k + 1) * blk] = hi
            split[i, blk : 2 * blk, k * blk : (k + 1) * blk] = (
                a - hi.astype(jnp.float32)
            ).astype(jnp.bfloat16)

    first_half = nb // 2

    @pl.loop(0, first_half)
    def _(i):
        pltpu.make_async_copy(mat_hbm.at[i], mat_in.at[i], mat_sem.at[i]).wait()
        make_split(i)

    pl.semaphore_wait(barrier, count)
    x_sends = [
        pltpu.make_async_remote_copy(
            src_ref=x_hbm,
            dst_ref=x_got.at[p],
            send_sem=xs_sem.at[p],
            recv_sem=xr_sem.at[p],
            device_id=(me_s, peer),
            device_id_type=MESH,
        )
        for p, peer in enumerate(net_peer)
    ]
    for copy in x_sends:
        copy.start()
    for copy in small:
        copy.wait()

    upper = lax.broadcasted_iota(jnp.int32, (R, blk), 0) < L

    def halves(v):
        hi = v.astype(jnp.bfloat16).astype(jnp.float32)
        return jnp.where(upper, hi, v - hi)

    for s in range(L):
        for r in (s, s + L):
            xv[pl.ds(r, nb, stride=R), :] = x_in[s]
            bv[pl.ds(r, nb, stride=R), :] = dem_in[s]
            dv[pl.ds(r, nb, stride=R), :] = cost_in[...] + lam_in[s]
            penb[pl.ds(r, nb, stride=R), :] = pen_in[...]
    for i in range(nb):
        sec_rows[i : i + 1, :] = jnp.full((1, blk), secs[i], jnp.int32)
        hl[HB + i] = halves(xv[i * R : (i + 1) * R, :])

    @pl.loop(first_half, nb)
    def _(i):
        pltpu.make_async_copy(mat_hbm.at[i], mat_in.at[i], mat_sem.at[i]).wait()
        make_split(i)

    for copy in x_sends:
        copy.wait()

    def halo_of_rows(ref, rows):
        return [
            jnp.concatenate([ref[s, r : r + 1] for s in list(range(L)) * 2], axis=0) for r in rows
        ]

    zero = jnp.zeros((R, blk), jnp.float32)

    def set_halo(low, high):
        for j in range(HB):
            hl[j] = halves(jnp.where(has_left, low[j], zero))
            hl[HB + nb + j] = halves(jnp.where(has_right, high[j], zero))

    if nets > 1:
        set_halo(
            halo_of_rows(x_got.at[0], range(nb - HB, nb)),
            halo_of_rows(x_got.at[nets - 2], range(HB)),
        )
    else:
        set_halo([zero] * HB, [zero] * HB)

    def forward_row(i):
        lhs = jnp.concatenate([hl[cols[k, i]] for k in range(nnz)], axis=1).astype(jnp.bfloat16)
        out = lax.dot_general(
            lhs, split[i], (((1,), (1,)), ((), ())), preferred_element_type=jnp.float32
        )
        both = out[:, :blk] + out[:, blk:]
        return both + pltpu.roll(both, L, 0)

    def transpose_row(i, w, acc):
        h = halves(w)
        lhs = jnp.concatenate([h, h], axis=1).astype(jnp.bfloat16)
        out = lax.dot_general(
            lhs, split[i], (((1,), (0,)), ((), ())), preferred_element_type=jnp.float32
        )
        both = out + pltpu.roll(out, L, 0)

        def put(at, term):
            acc[at] = term if acc[at] is None else acc[at] + term

        put(HB + i, both[:, :blk])
        for k in range(1, nnz):
            term = both[:, k * blk : (k + 1) * blk]
            for o in range(-HB, HB + 1):
                if o != 0:
                    put(HB + i + o, jnp.where(cols[k, i] == HB + i + o, term, zero))

    edge = list(range(HB)) + list(range(nb - HB, nb))
    inner = list(range(HB, nb - HB))

    def send(e, blocks, partial):
        for j, b in enumerate(blocks):
            if b is not None:
                msg_out[e, j] = b
        if partial is not None:
            msg_out[e, 2 * HB] = partial
        first = 0 if blocks else 2 * HB
        last = 2 * HB + (1 if partial is not None else 0)
        copies = [
            pltpu.make_async_remote_copy(
                src_ref=msg_out.at[e, pl.ds(first, last - first)],
                dst_ref=msg_in.at[e, p, pl.ds(first, last - first)],
                send_sem=ms_sem.at[e, p],
                recv_sem=mr_sem.at[e, p],
                device_id=(me_s, peer),
                device_id_type=MESH,
            )
            for p, peer in enumerate(net_peer)
        ]
        for copy in copies:
            copy.start()
        return copies

    def neighbours(e):
        if nets == 1:
            return [zero] * HB, [zero] * HB
        low = [jnp.where(has_left, msg_in[e, 0, HB + j], zero) for j in range(HB)]
        high = [jnp.where(has_right, msg_in[e, nets - 2, j], zero) for j in range(HB)]
        return low, high

    def total(e, partial):
        for p in range(nets - 1):
            partial = partial + msg_in[e, p, 2 * HB]
        return jnp.sum(partial, axis=1, keepdims=True)

    def wait(copies):
        for copy in copies:
            copy.wait()

    def transposed(e, w, partial):
        acc = [None] * (nb + 2 * HB)
        for i in edge:
            transpose_row(i, w[i], acc)
        copies = send(e, acc[:HB] + acc[HB + nb :], partial)
        for i in inner:
            transpose_row(i, w[i], acc)
        wait(copies)
        low, high = neighbours(e)
        z = acc[HB : HB + nb]
        for j in range(HB):
            z[j] = z[j] + low[j]
            z[nb - HB + j] = z[nb - HB + j] + high[j]
        return z

    def forward_with_halo(e, v, partial):
        copies = send(e, v[:HB] + v[nb - HB :], partial)
        for i in range(nb):
            hl[HB + i] = halves(v[i])
        w = [None] * nb
        for i in inner:
            w[i] = forward_row(i)
        wait(copies)
        low, high = neighbours(e)
        set_halo(low, high)
        for i in edge:
            w[i] = forward_row(i)
        return w

    def rows(ref):
        return [ref[i * R : (i + 1) * R, :] for i in range(nb)]

    def add_all(terms):
        while len(terms) > 1:
            terms = [
                terms[j] + terms[j + 1] if j + 1 < len(terms) else terms[j]
                for j in range(0, len(terms), 2)
            ]
        return terms[0]

    w = [bv[i * R : (i + 1) * R, :] - forward_row(i) for i in range(nb)]
    z = transposed(0, w, None)
    r0 = [z[i] - dv[i * R : (i + 1) * R, :] for i in range(nb)]
    part0 = add_all([v * v for v in r0])
    for i in range(nb):
        rv[i * R : (i + 1) * R, :] = r0[i]
    wa = forward_with_halo(1, r0, part0)
    norm0 = total(1, part0)
    for i in range(nb):
        w0[i * R : (i + 1) * R, :] = wa[i]
    pen = rows(penb)
    part_q = add_all(
        [p * v * v for p, v in zip(pen, rows(rv))] + [v * v for v in wa]
    )
    z = transposed(2, wa, part_q)
    a0 = norm0 / total(2, part_q)
    r0 = rows(rv)
    pen = rows(penb)
    r1 = [r0[i] - a0 * (pen[i] * r0[i] + z[i]) for i in range(nb)]
    part1 = add_all([v * v for v in r1])
    for i in range(nb):
        dv[i * R : (i + 1) * R, :] = r1[i]
        bv[i * R : (i + 1) * R, :] = xv[i * R : (i + 1) * R, :] + a0 * r0[i]
    wb = forward_with_halo(3, r1, part1)
    norm1 = total(3, part1)
    beta = norm1 / norm0
    d1 = [dv[i * R : (i + 1) * R, :] + beta * rv[i * R : (i + 1) * R, :] for i in range(nb)]
    ad = [wb[i] + beta * w0[i * R : (i + 1) * R, :] for i in range(nb)]
    part_q = add_all(
        [penb[i * R : (i + 1) * R, :] * d1[i] * d1[i] for i in range(nb)] + [v * v for v in ad]
    )
    wait(send(4, [], part_q))
    a1 = norm1 / total(4, part_q)
    for i in range(nb):
        rows_i = slice(i * R, (i + 1) * R)
        xv[rows_i, :] = jnp.maximum(bv[rows_i, :] + a1 * d1[i], 0.0)

    clipped = [xv[pl.ds(s, nb, stride=R), :] for s in range(L)]
    group = jnp.right_shift(jnp.int32(L * nodes), sec_rows[...])
    sums = clipped
    for b in range(L.bit_length() - 1):
        sums = [
            sums[s] + jnp.where(group > (1 << b), sums[s ^ (1 << b)], 0.0) for s in range(L)
        ]
    mine = sums[0]
    base = mine
    slot = 0
    for f, (at, masks) in enumerate(phases):
        sum_out[f] = mine
        copies = []
        for j, mask in enumerate(masks):
            copies.append(
                pltpu.make_async_remote_copy(
                    src_ref=sum_out.at[f],
                    dst_ref=sum_in.at[slot + j],
                    send_sem=ss_sem.at[slot + j],
                    recv_sem=sr_sem.at[slot + j],
                    device_id=(scen_peer(at, mask), me_n),
                    device_id_type=MESH,
                )
            )
        for copy in copies:
            copy.start()
        wait(copies)
        got = [sum_in[slot + j] for j in range(len(masks))]
        extra = jnp.where(group > (L << at), got[0], 0.0)
        if len(masks) == 3:
            extra = extra + jnp.where(group > (L << (at + 1)), got[1] + got[2], 0.0)
        mine = mine + extra
        slot += len(masks)
    shared = group >= L
    size = group.astype(jnp.float32)
    for s in range(L):
        mean = jnp.where(shared, mine, sums[s]) / size
        cons_ref[s] = mean
        newm_ref[s] = lam_in[s] + pen_in[...] * (clipped[s] - mean)


def body(*args):
    x = args[0]
    mat = args[5]
    L, nb, blk = x.shape
    nnz = mat.shape[1]
    nets = lax.axis_size("net")
    nodes = lax.axis_size("scen")
    R = 2 * L
    others = max(nets - 1, 1)
    phases = phases_of(nodes)
    slots = max(sum(len(m) for _, m in phases), 1)
    f32 = jnp.float32
    V = pltpu.VMEM
    dma = pltpu.SemaphoreType.DMA
    scratch = [
        V((L, nb, blk), f32),
        V((L, nb, blk), f32),
        V((L, nb, blk), f32),
        V((nb, blk), f32),
        V((nb, blk), f32),
        V(mat.shape, f32),
        pltpu.SMEM((nnz, nb), jnp.int32),
        pltpu.SMEM((nb,), jnp.int32),
        V((nb, 2 * blk, nnz * blk), jnp.bfloat16),
        V((nb * R, blk), f32),
        V((nb * R, blk), f32),
        V((nb * R, blk), f32),
        V((nb * R, blk), f32),
        V((nb + 2 * HB, R, blk), f32),
        V((nb * R, blk), f32),
        V((nb * R, blk), f32),
        V((nb, blk), jnp.int32),
        V((others, L, nb, blk), f32),
        V((5, 2 * HB + 1, R, blk), f32),
        V((5, others, 2 * HB + 1, R, blk), f32),
        V((max(len(phases), 1), nb, blk), f32),
        V((slots, nb, blk), f32),
        dma((7,)),
        dma((nb,)),
        dma((others,)),
        dma((others,)),
        dma((5, others)),
        dma((5, others)),
        dma((slots,)),
        dma((slots,)),
    ]
    hbm_spec = pl.BlockSpec(memory_space=pltpu.HBM)
    vmem_spec = pl.BlockSpec(memory_space=pltpu.VMEM)
    return pl.pallas_call(
        functools.partial(kernel, nets, nodes),
        out_shape=(jax.ShapeDtypeStruct(x.shape, f32), jax.ShapeDtypeStruct(x.shape, f32)),
        in_specs=[hbm_spec] * 8,
        out_specs=(vmem_spec, vmem_spec),
        scratch_shapes=scratch,
        compiler_params=pltpu.CompilerParams(
            collective_id=0, has_side_effects=True, vmem_limit_bytes=67_043_328
        ),
    )(*args[:6], args[6].T, args[7])


def solution(mesh):
    placed = (
        P("scen", "net", None),
        P("scen", "net", None),
        P("scen", "net", None),
        P("net", None),
        P("net", None),
        P("net", None, None, None),
        P("net", None),
        P("net"),
    )
    fn = jax.shard_map(
        body,
        mesh=mesh,
        in_specs=placed,
        out_specs=(P("scen", "net", None), P("scen", "net", None)),
        check_vma=False,
    )
    return lambda *args: tuple(fn(*args))
```

```python
import functools

import jax
import jax.numpy as jnp
from jax import lax
from jax.experimental import pallas as pl
from jax.experimental.pallas import tpu as pltpu
from jax.sharding import PartitionSpec as P

HB = 2
MESH = pl.DeviceIdType.MESH


def phases_of(nodes):
    bits = nodes.bit_length() - 1
    out = []
    at = 0
    while at < bits:
        take = min(2, bits - at)
        out.append((at, [m << at for m in range(1, 1 << take)]))
        at += take
    return out


def kernel(
    nets,
    nodes,
    x_hbm,
    lam_hbm,
    dem_hbm,
    cost_hbm,
    pen_hbm,
    mat_hbm,
    col_hbm,
    sec_hbm,
    sum_ref,
    clip_ref,
    size_ref,
    x_in,
    lam_in,
    dem_in,
    cost_in,
    pen_in,
    mat_in,
    cols,
    secs,
    split,
    xv,
    bv,
    dv,
    penb,
    hl,
    rv,
    w0,
    sec_rows,
    x_got,
    msg_out,
    msg_in,
    sum_out,
    sum_in,
    in_sem,
    mat_sem,
    xs_sem,
    xr_sem,
    ms_sem,
    mr_sem,
    ss_sem,
    sr_sem,
):
    L, nb, blk = x_in.shape
    nnz = mat_in.shape[1]
    R = 2 * L
    me_s = lax.axis_index("scen")
    me_n = lax.axis_index("net")
    phases = phases_of(nodes)

    small = [
        pltpu.make_async_copy(src, dst, in_sem.at[j])
        for j, (src, dst) in enumerate(
            [
                (x_hbm, x_in),
                (col_hbm, cols),
                (dem_hbm, dem_in),
                (lam_hbm, lam_in),
                (cost_hbm, cost_in),
                (pen_hbm, pen_in),
                (sec_hbm, secs),
            ]
        )
    ]
    for copy in small:
        copy.start()
    mats = [pltpu.make_async_copy(mat_hbm.at[i], mat_in.at[i], mat_sem.at[i]) for i in range(nb)]
    for copy in mats:
        copy.start()

    net_peer = [lax.rem(me_n + p, nets) for p in range(1, nets)]
    barrier = pltpu.get_barrier_semaphore()
    count = 0
    for peer in net_peer:
        pl.semaphore_signal(barrier, inc=1, device_id=(me_s, peer), device_id_type=MESH)
        count += 1

    def scen_peer(at, mask):
        bit = mask >> at
        low = lax.rem(me_s // (1 << at), 2)
        flipped = me_s
        if bit & 1:
            flipped = flipped + (1 - 2 * low) * (1 << at)
        if bit & 2:
            high = lax.rem(me_s // (2 << at), 2)
            flipped = flipped + (1 - 2 * high) * (2 << at)
        return flipped

    for at, masks in phases:
        for mask in masks:
            pl.semaphore_signal(
                barrier, inc=1, device_id=(scen_peer(at, mask), me_n), device_id_type=MESH
            )
            count += 1

    has_left = me_n > 0
    has_right = me_n < nets - 1

    def make_split(i):
        for k in range(nnz):
            a = mat_in[i, k]
            hi = a.astype(jnp.bfloat16)
            split[i, 0:blk, k * blk : (k + 1) * blk] = hi
            split[i, blk : 2 * blk, k * blk : (k + 1) * blk] = (
                a - hi.astype(jnp.float32)
            ).astype(jnp.bfloat16)

    first_half = nb // 2

    @pl.loop(0, first_half)
    def _(i):
        pltpu.make_async_copy(mat_hbm.at[i], mat_in.at[i], mat_sem.at[i]).wait()
        make_split(i)

    pl.semaphore_wait(barrier, count)
    x_sends = [
        pltpu.make_async_remote_copy(
            src_ref=x_hbm,
            dst_ref=x_got.at[p],
            send_sem=xs_sem.at[p],
            recv_sem=xr_sem.at[p],
            device_id=(me_s, peer),
            device_id_type=MESH,
        )
        for p, peer in enumerate(net_peer)
    ]
    for copy in x_sends:
        copy.start()
    for copy in small:
        copy.wait()

    upper = lax.broadcasted_iota(jnp.int32, (R, blk), 0) < L

    def halves(v):
        hi = v.astype(jnp.bfloat16).astype(jnp.float32)
        return jnp.where(upper, hi, v - hi)

    for s in range(L):
        for r in (s, s + L):
            xv[pl.ds(r, nb, stride=R), :] = x_in[s]
            bv[pl.ds(r, nb, stride=R), :] = dem_in[s]
            dv[pl.ds(r, nb, stride=R), :] = cost_in[...] + lam_in[s]
            penb[pl.ds(r, nb, stride=R), :] = pen_in[...]
    for i in range(nb):
        sec_rows[i : i + 1, :] = jnp.full((1, blk), secs[i], jnp.int32)
        hl[HB + i] = halves(xv[i * R : (i + 1) * R, :])

    @pl.loop(first_half, nb)
    def _(i):
        pltpu.make_async_copy(mat_hbm.at[i], mat_in.at[i], mat_sem.at[i]).wait()
        make_split(i)

    for copy in x_sends:
        copy.wait()

    def halo_of_rows(ref, rows):
        return [
            jnp.concatenate([ref[s, r : r + 1] for s in list(range(L)) * 2], axis=0) for r in rows
        ]

    zero = jnp.zeros((R, blk), jnp.float32)

    def set_halo(low, high):
        for j in range(HB):
            hl[j] = halves(jnp.where(has_left, low[j], zero))
            hl[HB + nb + j] = halves(jnp.where(has_right, high[j], zero))

    if nets > 1:
        set_halo(
            halo_of_rows(x_got.at[0], range(nb - HB, nb)),
            halo_of_rows(x_got.at[nets - 2], range(HB)),
        )
    else:
        set_halo([zero] * HB, [zero] * HB)

    def forward_row(i):
        lhs = jnp.concatenate([hl[cols[k, i]] for k in range(nnz)], axis=1).astype(jnp.bfloat16)
        out = lax.dot_general(
            lhs, split[i], (((1,), (1,)), ((), ())), preferred_element_type=jnp.float32
        )
        both = out[:, :blk] + out[:, blk:]
        return both + pltpu.roll(both, L, 0)

    def transpose_row(i, w, acc):
        h = halves(w)
        lhs = jnp.concatenate([h, h], axis=1).astype(jnp.bfloat16)
        out = lax.dot_general(
            lhs, split[i], (((1,), (0,)), ((), ())), preferred_element_type=jnp.float32
        )
        both = out + pltpu.roll(out, L, 0)

        def put(at, term):
            acc[at] = term if acc[at] is None else acc[at] + term

        put(HB + i, both[:, :blk])
        for k in range(1, nnz):
            term = both[:, k * blk : (k + 1) * blk]
            for o in range(-HB, HB + 1):
                if o != 0:
                    put(HB + i + o, jnp.where(cols[k, i] == HB + i + o, term, zero))

    edge = list(range(HB)) + list(range(nb - HB, nb))
    inner = list(range(HB, nb - HB))

    def send(e, blocks, partial):
        for j, b in enumerate(blocks):
            if b is not None:
                msg_out[e, j] = b
        if partial is not None:
            msg_out[e, 2 * HB] = partial
        first = 0 if blocks else 2 * HB
        last = 2 * HB + (1 if partial is not None else 0)
        copies = [
            pltpu.make_async_remote_copy(
                src_ref=msg_out.at[e, pl.ds(first, last - first)],
                dst_ref=msg_in.at[e, p, pl.ds(first, last - first)],
                send_sem=ms_sem.at[e, p],
                recv_sem=mr_sem.at[e, p],
                device_id=(me_s, peer),
                device_id_type=MESH,
            )
            for p, peer in enumerate(net_peer)
        ]
        for copy in copies:
            copy.start()
        return copies

    def neighbours(e):
        if nets == 1:
            return [zero] * HB, [zero] * HB
        low = [jnp.where(has_left, msg_in[e, 0, HB + j], zero) for j in range(HB)]
        high = [jnp.where(has_right, msg_in[e, nets - 2, j], zero) for j in range(HB)]
        return low, high

    def total(e, partial):
        for p in range(nets - 1):
            partial = partial + msg_in[e, p, 2 * HB]
        return jnp.sum(partial, axis=1, keepdims=True)

    def wait(copies):
        for copy in copies:
            copy.wait()

    def transposed(e, w, partial):
        acc = [None] * (nb + 2 * HB)
        for i in edge:
            transpose_row(i, w[i], acc)
        copies = send(e, acc[:HB] + acc[HB + nb :], partial)
        for i in inner:
            transpose_row(i, w[i], acc)
        wait(copies)
        low, high = neighbours(e)
        z = acc[HB : HB + nb]
        for j in range(HB):
            z[j] = z[j] + low[j]
            z[nb - HB + j] = z[nb - HB + j] + high[j]
        return z

    def forward_with_halo(e, v, partial):
        copies = send(e, v[:HB] + v[nb - HB :], partial)
        for i in range(nb):
            hl[HB + i] = halves(v[i])
        w = [None] * nb
        for i in inner:
            w[i] = forward_row(i)
        wait(copies)
        low, high = neighbours(e)
        set_halo(low, high)
        for i in edge:
            w[i] = forward_row(i)
        return w

    def rows(ref):
        return [ref[i * R : (i + 1) * R, :] for i in range(nb)]

    def add_all(terms):
        while len(terms) > 1:
            terms = [
                terms[j] + terms[j + 1] if j + 1 < len(terms) else terms[j]
                for j in range(0, len(terms), 2)
            ]
        return terms[0]

    w = [bv[i * R : (i + 1) * R, :] - forward_row(i) for i in range(nb)]
    z = transposed(0, w, None)
    r0 = [z[i] - dv[i * R : (i + 1) * R, :] for i in range(nb)]
    part0 = add_all([v * v for v in r0])
    for i in range(nb):
        rv[i * R : (i + 1) * R, :] = r0[i]
    wa = forward_with_halo(1, r0, part0)
    norm0 = total(1, part0)
    for i in range(nb):
        w0[i * R : (i + 1) * R, :] = wa[i]
    pen = rows(penb)
    part_q = add_all(
        [p * v * v for p, v in zip(pen, rows(rv))] + [v * v for v in wa]
    )
    z = transposed(2, wa, part_q)
    a0 = norm0 / total(2, part_q)
    r0 = rows(rv)
    pen = rows(penb)
    r1 = [r0[i] - a0 * (pen[i] * r0[i] + z[i]) for i in range(nb)]
    part1 = add_all([v * v for v in r1])
    for i in range(nb):
        dv[i * R : (i + 1) * R, :] = r1[i]
        bv[i * R : (i + 1) * R, :] = xv[i * R : (i + 1) * R, :] + a0 * r0[i]
    wb = forward_with_halo(3, r1, part1)
    norm1 = total(3, part1)
    beta = norm1 / norm0
    d1 = [dv[i * R : (i + 1) * R, :] + beta * rv[i * R : (i + 1) * R, :] for i in range(nb)]
    ad = [wb[i] + beta * w0[i * R : (i + 1) * R, :] for i in range(nb)]
    part_q = add_all(
        [penb[i * R : (i + 1) * R, :] * d1[i] * d1[i] for i in range(nb)] + [v * v for v in ad]
    )
    wait(send(4, [], part_q))
    a1 = norm1 / total(4, part_q)
    for i in range(nb):
        rows_i = slice(i * R, (i + 1) * R)
        xv[rows_i, :] = jnp.maximum(bv[rows_i, :] + a1 * d1[i], 0.0)

    clipped = [xv[pl.ds(s, nb, stride=R), :] for s in range(L)]
    group = jnp.right_shift(jnp.int32(L * nodes), sec_rows[...])
    sums = clipped
    for b in range(L.bit_length() - 1):
        sums = [
            sums[s] + jnp.where(group > (1 << b), sums[s ^ (1 << b)], 0.0) for s in range(L)
        ]
    mine = sums[0]
    base = mine
    slot = 0
    for f, (at, masks) in enumerate(phases):
        sum_out[f] = mine
        copies = []
        for j, mask in enumerate(masks):
            copies.append(
                pltpu.make_async_remote_copy(
                    src_ref=sum_out.at[f],
                    dst_ref=sum_in.at[slot + j],
                    send_sem=ss_sem.at[slot + j],
                    recv_sem=sr_sem.at[slot + j],
                    device_id=(scen_peer(at, mask), me_n),
                    device_id_type=MESH,
                )
            )
        for copy in copies:
            copy.start()
        wait(copies)
        got = [sum_in[slot + j] for j in range(len(masks))]
        extra = jnp.where(group > (L << at), got[0], 0.0)
        if len(masks) == 3:
            extra = extra + jnp.where(group > (L << (at + 1)), got[1] + got[2], 0.0)
        mine = mine + extra
        slot += len(masks)
    shared = group >= L
    for s in range(L):
        sum_ref[s] = jnp.where(shared, mine, sums[s])
        clip_ref[s] = clipped[s]
    size_ref[...] = group.astype(jnp.float32)


def body(*args):
    x = args[0]
    mat = args[5]
    L, nb, blk = x.shape
    nnz = mat.shape[1]
    nets = lax.axis_size("net")
    nodes = lax.axis_size("scen")
    R = 2 * L
    others = max(nets - 1, 1)
    phases = phases_of(nodes)
    slots = max(sum(len(m) for _, m in phases), 1)
    f32 = jnp.float32
    V = pltpu.VMEM
    dma = pltpu.SemaphoreType.DMA
    scratch = [
        V((L, nb, blk), f32),
        V((L, nb, blk), f32),
        V((L, nb, blk), f32),
        V((nb, blk), f32),
        V((nb, blk), f32),
        V(mat.shape, f32),
        pltpu.SMEM((nnz, nb), jnp.int32),
        pltpu.SMEM((nb,), jnp.int32),
        V((nb, 2 * blk, nnz * blk), jnp.bfloat16),
        V((nb * R, blk), f32),
        V((nb * R, blk), f32),
        V((nb * R, blk), f32),
        V((nb * R, blk), f32),
        V((nb + 2 * HB, R, blk), f32),
        V((nb * R, blk), f32),
        V((nb * R, blk), f32),
        V((nb, blk), jnp.int32),
        V((others, L, nb, blk), f32),
        V((5, 2 * HB + 1, R, blk), f32),
        V((5, others, 2 * HB + 1, R, blk), f32),
        V((max(len(phases), 1), nb, blk), f32),
        V((slots, nb, blk), f32),
        dma((7,)),
        dma((nb,)),
        dma((others,)),
        dma((others,)),
        dma((5, others)),
        dma((5, others)),
        dma((slots,)),
        dma((slots,)),
    ]
    hbm_spec = pl.BlockSpec(memory_space=pltpu.HBM)
    vmem_spec = pl.BlockSpec(memory_space=pltpu.VMEM)
    sums, clipped, size = pl.pallas_call(
        functools.partial(kernel, nets, nodes),
        out_shape=(V(x.shape, f32), V(x.shape, f32), V((nb, blk), f32)),
        in_specs=[hbm_spec] * 8,
        out_specs=(vmem_spec, vmem_spec, vmem_spec),
        scratch_shapes=scratch,
        compiler_params=pltpu.CompilerParams(
            collective_id=0, has_side_effects=True, vmem_limit_bytes=60_000_000
        ),
    )(*args[:6], args[6].T, args[7])
    mean = sums / size[None]
    return mean, args[1] + args[4][None] * (clipped - mean)


def solution(mesh):
    placed = (
        P("scen", "net", None),
        P("scen", "net", None),
        P("scen", "net", None),
        P("net", None),
        P("net", None),
        P("net", None, None, None),
        P("net", None),
        P("net"),
    )
    fn = jax.shard_map(
        body,
        mesh=mesh,
        in_specs=placed,
        out_specs=(P("scen", "net", None), P("scen", "net", None)),
        check_vma=False,
    )
    return lambda *args: tuple(fn(*args))
```

```python
import functools

import jax
import jax.numpy as jnp
from jax import lax
from jax.experimental import pallas as pl
from jax.experimental.pallas import tpu as pltpu
from jax.sharding import PartitionSpec as P

HB = 2
MESH = pl.DeviceIdType.MESH


def phases_of(nodes):
    bits = nodes.bit_length() - 1
    out = []
    at = 0
    while at < bits:
        take = min(2, bits - at)
        out.append((at, [m << at for m in range(1, 1 << take)]))
        at += take
    return out


def kernel(
    nets,
    nodes,
    x_hbm,
    lam_hbm,
    dem_hbm,
    cost_hbm,
    pen_hbm,
    mat_hbm,
    col_hbm,
    sec_hbm,
    sum_ref,
    clip_ref,
    size_ref,
    x_in,
    lam_in,
    dem_in,
    cost_in,
    pen_in,
    mat_in,
    cols,
    secs,
    split,
    xv,
    bv,
    dv,
    penb,
    hl,
    rv,
    w0,
    sec_rows,
    x_got,
    msg_out,
    msg_in,
    sum_out,
    sum_in,
    in_sem,
    mat_sem,
    xs_sem,
    xr_sem,
    ms_sem,
    mr_sem,
    ss_sem,
    sr_sem,
):
    L, nb, blk = x_in.shape
    nnz = mat_in.shape[1]
    R = 2 * L
    me_s = lax.axis_index("scen")
    me_n = lax.axis_index("net")
    phases = phases_of(nodes)

    small = [
        pltpu.make_async_copy(src, dst, in_sem.at[j])
        for j, (src, dst) in enumerate(
            [
                (x_hbm, x_in),
                (col_hbm, cols),
                (dem_hbm, dem_in),
                (lam_hbm, lam_in),
                (cost_hbm, cost_in),
                (pen_hbm, pen_in),
                (sec_hbm, secs),
            ]
        )
    ]
    for copy in small:
        copy.start()
    mats = [pltpu.make_async_copy(mat_hbm.at[i], mat_in.at[i], mat_sem.at[i]) for i in range(nb)]
    for copy in mats:
        copy.start()

    net_peer = [lax.rem(me_n + p, nets) for p in range(1, nets)]
    barrier = pltpu.get_barrier_semaphore()
    count = 0
    for peer in net_peer:
        pl.semaphore_signal(barrier, inc=1, device_id=(me_s, peer), device_id_type=MESH)
        count += 1

    def scen_peer(at, mask):
        bit = mask >> at
        low = lax.rem(me_s // (1 << at), 2)
        flipped = me_s
        if bit & 1:
            flipped = flipped + (1 - 2 * low) * (1 << at)
        if bit & 2:
            high = lax.rem(me_s // (2 << at), 2)
            flipped = flipped + (1 - 2 * high) * (2 << at)
        return flipped

    for at, masks in phases:
        for mask in masks:
            pl.semaphore_signal(
                barrier, inc=1, device_id=(scen_peer(at, mask), me_n), device_id_type=MESH
            )
            count += 1

    has_left = me_n > 0
    has_right = me_n < nets - 1

    def make_split(i):
        for k in range(nnz):
            a = mat_in[i, k]
            hi = a.astype(jnp.bfloat16)
            split[i, 0:blk, k * blk : (k + 1) * blk] = hi
            split[i, blk : 2 * blk, k * blk : (k + 1) * blk] = (
                a - hi.astype(jnp.float32)
            ).astype(jnp.bfloat16)

    half = nb // 2
    for copy in small:
        copy.wait()

    upper = lax.broadcasted_iota(jnp.int32, (R, blk), 0) < L

    def halves(v):
        hi = v.astype(jnp.bfloat16).astype(jnp.float32)
        return jnp.where(upper, hi, v - hi)

    for s in range(L):
        for r in (s, s + L):
            xv[pl.ds(r, nb, stride=R), :] = x_in[s]
            bv[pl.ds(r, nb, stride=R), :] = dem_in[s]
            dv[pl.ds(r, nb, stride=R), :] = cost_in[...] + lam_in[s]
            penb[pl.ds(r, nb, stride=R), :] = pen_in[...]
    for i in range(nb):
        sec_rows[i : i + 1, :] = jnp.full((1, blk), secs[i], jnp.int32)
        hl[HB + i] = halves(xv[i * R : (i + 1) * R, :])

    def halo_of_rows(ref, rows):
        return [
            jnp.concatenate([ref[s, r : r + 1] for s in list(range(L)) * 2], axis=0) for r in rows
        ]

    zero = jnp.zeros((R, blk), jnp.float32)

    def set_halo(low, high):
        for j in range(HB):
            hl[j] = halves(jnp.where(has_left, low[j], zero))
            hl[HB + nb + j] = halves(jnp.where(has_right, high[j], zero))

    def forward_row(i):
        lhs = jnp.concatenate([hl[cols[k, i]] for k in range(nnz)], axis=1).astype(jnp.bfloat16)
        out = lax.dot_general(
            lhs, split[i], (((1,), (1,)), ((), ())), preferred_element_type=jnp.float32
        )
        both = out[:, :blk] + out[:, blk:]
        return both + pltpu.roll(both, L, 0)

    edge = list(range(HB)) + list(range(nb - HB, nb))
    inner = list(range(HB, nb - HB))

    w = [None] * nb

    def first_product(rows_now):
        for i in rows_now:
            w[i] = bv[i * R : (i + 1) * R, :] - forward_row(i)

    @pl.loop(0, half)
    def _(i):
        pltpu.make_async_copy(mat_hbm.at[i], mat_in.at[i], mat_sem.at[i]).wait()
        make_split(i)

    first_product([i for i in inner if i < half])
    pl.semaphore_wait(barrier, count)
    x_sends = [
        pltpu.make_async_remote_copy(
            src_ref=x_hbm,
            dst_ref=x_got.at[p],
            send_sem=xs_sem.at[p],
            recv_sem=xr_sem.at[p],
            device_id=(me_s, peer),
            device_id_type=MESH,
        )
        for p, peer in enumerate(net_peer)
    ]
    for copy in x_sends:
        copy.start()
    @pl.loop(half, nb)
    def _(i):
        pltpu.make_async_copy(mat_hbm.at[i], mat_in.at[i], mat_sem.at[i]).wait()
        make_split(i)

    first_product([i for i in inner if i >= half])
    for copy in x_sends:
        copy.wait()
    if nets > 1:
        set_halo(
            halo_of_rows(x_got.at[0], range(nb - HB, nb)),
            halo_of_rows(x_got.at[nets - 2], range(HB)),
        )
    else:
        set_halo([zero] * HB, [zero] * HB)

    first_product(edge)

    def transpose_row(i, w, acc):
        h = halves(w)
        lhs = jnp.concatenate([h, h], axis=1).astype(jnp.bfloat16)
        out = lax.dot_general(
            lhs, split[i], (((1,), (0,)), ((), ())), preferred_element_type=jnp.float32
        )
        both = out + pltpu.roll(out, L, 0)

        def put(at, term):
            acc[at] = term if acc[at] is None else acc[at] + term

        put(HB + i, both[:, :blk])
        for k in range(1, nnz):
            term = both[:, k * blk : (k + 1) * blk]
            for o in range(-HB, HB + 1):
                if o != 0:
                    put(HB + i + o, jnp.where(cols[k, i] == HB + i + o, term, zero))

    def send(e, blocks, partial):
        for j, b in enumerate(blocks):
            if b is not None:
                msg_out[e, j] = b
        if partial is not None:
            msg_out[e, 2 * HB] = partial
        first = 0 if blocks else 2 * HB
        last = 2 * HB + (1 if partial is not None else 0)
        copies = [
            pltpu.make_async_remote_copy(
                src_ref=msg_out.at[e, pl.ds(first, last - first)],
                dst_ref=msg_in.at[e, p, pl.ds(first, last - first)],
                send_sem=ms_sem.at[e, p],
                recv_sem=mr_sem.at[e, p],
                device_id=(me_s, peer),
                device_id_type=MESH,
            )
            for p, peer in enumerate(net_peer)
        ]
        for copy in copies:
            copy.start()
        return copies

    def neighbours(e):
        if nets == 1:
            return [zero] * HB, [zero] * HB
        low = [jnp.where(has_left, msg_in[e, 0, HB + j], zero) for j in range(HB)]
        high = [jnp.where(has_right, msg_in[e, nets - 2, j], zero) for j in range(HB)]
        return low, high

    def total(e, partial):
        for p in range(nets - 1):
            partial = partial + msg_in[e, p, 2 * HB]
        return jnp.sum(partial, axis=1, keepdims=True)

    def wait(copies):
        for copy in copies:
            copy.wait()

    def transposed(e, w, partial):
        acc = [None] * (nb + 2 * HB)
        for i in edge:
            transpose_row(i, w[i], acc)
        copies = send(e, acc[:HB] + acc[HB + nb :], partial)
        for i in inner:
            transpose_row(i, w[i], acc)
        wait(copies)
        low, high = neighbours(e)
        z = acc[HB : HB + nb]
        for j in range(HB):
            z[j] = z[j] + low[j]
            z[nb - HB + j] = z[nb - HB + j] + high[j]
        return z

    def forward_with_halo(e, v, partial):
        copies = send(e, v[:HB] + v[nb - HB :], partial)
        for i in range(nb):
            hl[HB + i] = halves(v[i])
        w = [None] * nb
        for i in inner:
            w[i] = forward_row(i)
        wait(copies)
        low, high = neighbours(e)
        set_halo(low, high)
        for i in edge:
            w[i] = forward_row(i)
        return w

    def rows(ref):
        return [ref[i * R : (i + 1) * R, :] for i in range(nb)]

    def add_all(terms):
        while len(terms) > 1:
            terms = [
                terms[j] + terms[j + 1] if j + 1 < len(terms) else terms[j]
                for j in range(0, len(terms), 2)
            ]
        return terms[0]

    z = transposed(0, w, None)
    r0 = [z[i] - dv[i * R : (i + 1) * R, :] for i in range(nb)]
    part0 = add_all([v * v for v in r0])
    for i in range(nb):
        rv[i * R : (i + 1) * R, :] = r0[i]
    wa = forward_with_halo(1, r0, part0)
    norm0 = total(1, part0)
    for i in range(nb):
        w0[i * R : (i + 1) * R, :] = wa[i]
    pen = rows(penb)
    part_q = add_all(
        [p * v * v for p, v in zip(pen, rows(rv))] + [v * v for v in wa]
    )
    z = transposed(2, wa, part_q)
    a0 = norm0 / total(2, part_q)
    r0 = rows(rv)
    pen = rows(penb)
    r1 = [r0[i] - a0 * (pen[i] * r0[i] + z[i]) for i in range(nb)]
    part1 = add_all([v * v for v in r1])
    for i in range(nb):
        dv[i * R : (i + 1) * R, :] = r1[i]
        bv[i * R : (i + 1) * R, :] = xv[i * R : (i + 1) * R, :] + a0 * r0[i]
    wb = forward_with_halo(3, r1, part1)
    norm1 = total(3, part1)
    beta = norm1 / norm0
    d1 = [dv[i * R : (i + 1) * R, :] + beta * rv[i * R : (i + 1) * R, :] for i in range(nb)]
    ad = [wb[i] + beta * w0[i * R : (i + 1) * R, :] for i in range(nb)]
    part_q = add_all(
        [penb[i * R : (i + 1) * R, :] * d1[i] * d1[i] for i in range(nb)] + [v * v for v in ad]
    )
    wait(send(4, [], part_q))
    a1 = norm1 / total(4, part_q)
    for i in range(nb):
        rows_i = slice(i * R, (i + 1) * R)
        xv[rows_i, :] = jnp.maximum(bv[rows_i, :] + a1 * d1[i], 0.0)

    clipped = [xv[pl.ds(s, nb, stride=R), :] for s in range(L)]
    group = jnp.right_shift(jnp.int32(L * nodes), sec_rows[...])
    sums = clipped
    for b in range(L.bit_length() - 1):
        sums = [
            sums[s] + jnp.where(group > (1 << b), sums[s ^ (1 << b)], 0.0) for s in range(L)
        ]
    mine = sums[0]
    base = mine
    slot = 0
    for f, (at, masks) in enumerate(phases):
        sum_out[f] = mine
        copies = []
        for j, mask in enumerate(masks):
            copies.append(
                pltpu.make_async_remote_copy(
                    src_ref=sum_out.at[f],
                    dst_ref=sum_in.at[slot + j],
                    send_sem=ss_sem.at[slot + j],
                    recv_sem=sr_sem.at[slot + j],
                    device_id=(scen_peer(at, mask), me_n),
                    device_id_type=MESH,
                )
            )
        for copy in copies:
            copy.start()
        wait(copies)
        got = [sum_in[slot + j] for j in range(len(masks))]
        extra = jnp.where(group > (L << at), got[0], 0.0)
        if len(masks) == 3:
            extra = extra + jnp.where(group > (L << (at + 1)), got[1] + got[2], 0.0)
        mine = mine + extra
        slot += len(masks)
    shared = group >= L
    for s in range(L):
        sum_ref[s] = jnp.where(shared, mine, sums[s])
        clip_ref[s] = clipped[s]
    size_ref[...] = group.astype(jnp.float32)


def body(*args):
    x = args[0]
    mat = args[5]
    L, nb, blk = x.shape
    nnz = mat.shape[1]
    nets = lax.axis_size("net")
    nodes = lax.axis_size("scen")
    R = 2 * L
    others = max(nets - 1, 1)
    phases = phases_of(nodes)
    slots = max(sum(len(m) for _, m in phases), 1)
    f32 = jnp.float32
    V = pltpu.VMEM
    dma = pltpu.SemaphoreType.DMA
    scratch = [
        V((L, nb, blk), f32),
        V((L, nb, blk), f32),
        V((L, nb, blk), f32),
        V((nb, blk), f32),
        V((nb, blk), f32),
        V(mat.shape, f32),
        pltpu.SMEM((nnz, nb), jnp.int32),
        pltpu.SMEM((nb,), jnp.int32),
        V((nb, 2 * blk, nnz * blk), jnp.bfloat16),
        V((nb * R, blk), f32),
        V((nb * R, blk), f32),
        V((nb * R, blk), f32),
        V((nb * R, blk), f32),
        V((nb + 2 * HB, R, blk), f32),
        V((nb * R, blk), f32),
        V((nb * R, blk), f32),
        V((nb, blk), jnp.int32),
        V((others, L, nb, blk), f32),
        V((5, 2 * HB + 1, R, blk), f32),
        V((5, others, 2 * HB + 1, R, blk), f32),
        V((max(len(phases), 1), nb, blk), f32),
        V((slots, nb, blk), f32),
        dma((7,)),
        dma((nb,)),
        dma((others,)),
        dma((others,)),
        dma((5, others)),
        dma((5, others)),
        dma((slots,)),
        dma((slots,)),
    ]
    hbm_spec = pl.BlockSpec(memory_space=pltpu.HBM)
    vmem_spec = pl.BlockSpec(memory_space=pltpu.VMEM)
    sums, clipped, size = pl.pallas_call(
        functools.partial(kernel, nets, nodes),
        out_shape=(V(x.shape, f32), V(x.shape, f32), V((nb, blk), f32)),
        in_specs=[hbm_spec] * 8,
        out_specs=(vmem_spec, vmem_spec, vmem_spec),
        scratch_shapes=scratch,
        compiler_params=pltpu.CompilerParams(
            collective_id=0, has_side_effects=True, vmem_limit_bytes=60_000_000
        ),
    )(*args[:6], args[6].T, args[7])
    mean = sums / size[None]
    return mean, args[1] + args[4][None] * (clipped - mean)


def solution(mesh):
    placed = (
        P("scen", "net", None),
        P("scen", "net", None),
        P("scen", "net", None),
        P("net", None),
        P("net", None),
        P("net", None, None, None),
        P("net", None),
        P("net"),
    )
    fn = jax.shard_map(
        body,
        mesh=mesh,
        in_specs=placed,
        out_specs=(P("scen", "net", None), P("scen", "net", None)),
        check_vma=False,
    )
    return lambda *args: tuple(fn(*args))
```

```python
import functools

import jax
import jax.numpy as jnp
from jax import lax
from jax.experimental import pallas as pl
from jax.experimental.pallas import tpu as pltpu
from jax.sharding import PartitionSpec as P

HB = 2
MESH = pl.DeviceIdType.MESH


def phases_of(nodes):
    bits = nodes.bit_length() - 1
    out = []
    at = 0
    while at < bits:
        take = min(2, bits - at)
        out.append((at, [m << at for m in range(1, 1 << take)]))
        at += take
    return out


def kernel(
    nets,
    nodes,
    x_hbm,
    lam_hbm,
    dem_hbm,
    cost_hbm,
    pen_hbm,
    mat_hbm,
    col_hbm,
    sec_hbm,
    sum_ref,
    clip_ref,
    size_ref,
    x_in,
    lam_in,
    dem_in,
    cost_in,
    pen_in,
    mat_in,
    cols,
    secs,
    split,
    xv,
    bv,
    dv,
    penb,
    hl,
    rv,
    w0,
    sec_rows,
    x_got,
    msg_out,
    msg_in,
    sum_out,
    sum_in,
    in_sem,
    mat_sem,
    xs_sem,
    xr_sem,
    ms_sem,
    mr_sem,
    ss_sem,
    sr_sem,
):
    L, nb, blk = x_in.shape
    nnz = mat_in.shape[1]
    R = 2 * L
    me_s = lax.axis_index("scen")
    me_n = lax.axis_index("net")
    phases = phases_of(nodes)

    small = [
        pltpu.make_async_copy(src, dst, in_sem.at[j])
        for j, (src, dst) in enumerate(
            [
                (x_hbm, x_in),
                (col_hbm, cols),
                (dem_hbm, dem_in),
                (lam_hbm, lam_in),
                (cost_hbm, cost_in),
                (pen_hbm, pen_in),
                (sec_hbm, secs),
            ]
        )
    ]
    for copy in small:
        copy.start()
    mats = [pltpu.make_async_copy(mat_hbm.at[i], mat_in.at[i], mat_sem.at[i]) for i in range(nb)]
    for copy in mats:
        copy.start()

    net_peer = [lax.rem(me_n + p, nets) for p in range(1, nets)]
    barrier = pltpu.get_barrier_semaphore()
    count = 0
    for peer in net_peer:
        pl.semaphore_signal(barrier, inc=1, device_id=(me_s, peer), device_id_type=MESH)
        count += 1

    def scen_peer(at, mask):
        bit = mask >> at
        low = lax.rem(me_s // (1 << at), 2)
        flipped = me_s
        if bit & 1:
            flipped = flipped + (1 - 2 * low) * (1 << at)
        if bit & 2:
            high = lax.rem(me_s // (2 << at), 2)
            flipped = flipped + (1 - 2 * high) * (2 << at)
        return flipped

    for at, masks in phases:
        for mask in masks:
            pl.semaphore_signal(
                barrier, inc=1, device_id=(scen_peer(at, mask), me_n), device_id_type=MESH
            )
            count += 1

    has_left = me_n > 0
    has_right = me_n < nets - 1

    def make_split(i):
        for k in range(nnz):
            a = mat_in[i, k]
            hi = a.astype(jnp.bfloat16)
            split[i, 0:blk, k * blk : (k + 1) * blk] = hi
            split[i, blk : 2 * blk, k * blk : (k + 1) * blk] = (
                a - hi.astype(jnp.float32)
            ).astype(jnp.bfloat16)

    pl.semaphore_wait(barrier, count)
    x_sends = [
        pltpu.make_async_remote_copy(
            src_ref=x_hbm,
            dst_ref=x_got.at[p],
            send_sem=xs_sem.at[p],
            recv_sem=xr_sem.at[p],
            device_id=(me_s, peer),
            device_id_type=MESH,
        )
        for p, peer in enumerate(net_peer)
    ]
    for copy in x_sends:
        copy.start()
    for copy in small:
        copy.wait()

    upper = lax.broadcasted_iota(jnp.int32, (R, blk), 0) < L

    def halves(v):
        hi = v.astype(jnp.bfloat16).astype(jnp.float32)
        return jnp.where(upper, hi, v - hi)

    for s in range(L):
        for r in (s, s + L):
            xv[pl.ds(r, nb, stride=R), :] = x_in[s]
            bv[pl.ds(r, nb, stride=R), :] = dem_in[s]
            dv[pl.ds(r, nb, stride=R), :] = cost_in[...] + lam_in[s]
            penb[pl.ds(r, nb, stride=R), :] = pen_in[...]
    for i in range(nb):
        sec_rows[i : i + 1, :] = jnp.full((1, blk), secs[i], jnp.int32)
        hl[HB + i] = halves(xv[i * R : (i + 1) * R, :])

    @pl.loop(0, nb)
    def _(i):
        pltpu.make_async_copy(mat_hbm.at[i], mat_in.at[i], mat_sem.at[i]).wait()
        make_split(i)

    for copy in x_sends:
        copy.wait()

    def halo_of_rows(ref, rows):
        return [
            jnp.concatenate([ref[s, r : r + 1] for s in list(range(L)) * 2], axis=0) for r in rows
        ]

    zero = jnp.zeros((R, blk), jnp.float32)

    def set_halo(low, high):
        for j in range(HB):
            hl[j] = halves(jnp.where(has_left, low[j], zero))
            hl[HB + nb + j] = halves(jnp.where(has_right, high[j], zero))

    if nets > 1:
        set_halo(
            halo_of_rows(x_got.at[0], range(nb - HB, nb)),
            halo_of_rows(x_got.at[nets - 2], range(HB)),
        )
    else:
        set_halo([zero] * HB, [zero] * HB)

    def forward_row(i):
        lhs = jnp.concatenate([hl[cols[k, i]] for k in range(nnz)], axis=1).astype(jnp.bfloat16)
        out = lax.dot_general(
            lhs, split[i], (((1,), (1,)), ((), ())), preferred_element_type=jnp.float32
        )
        both = out[:, :blk] + out[:, blk:]
        return both + pltpu.roll(both, L, 0)

    def transpose_row(i, w, acc):
        h = halves(w)
        lhs = jnp.concatenate([h, h], axis=1).astype(jnp.bfloat16)
        out = lax.dot_general(
            lhs, split[i], (((1,), (0,)), ((), ())), preferred_element_type=jnp.float32
        )
        both = out + pltpu.roll(out, L, 0)

        def put(at, term):
            acc[at] = term if acc[at] is None else acc[at] + term

        put(HB + i, both[:, :blk])
        for k in range(1, nnz):
            term = both[:, k * blk : (k + 1) * blk]
            for o in range(-HB, HB + 1):
                if o != 0:
                    put(HB + i + o, jnp.where(cols[k, i] == HB + i + o, term, zero))

    edge = list(range(HB)) + list(range(nb - HB, nb))
    inner = list(range(HB, nb - HB))

    def send(e, blocks, partial):
        for j, b in enumerate(blocks):
            if b is not None:
                msg_out[e, j] = b
        if partial is not None:
            msg_out[e, 2 * HB] = partial
        first = 0 if blocks else 2 * HB
        last = 2 * HB + (1 if partial is not None else 0)
        copies = [
            pltpu.make_async_remote_copy(
                src_ref=msg_out.at[e, pl.ds(first, last - first)],
                dst_ref=msg_in.at[e, p, pl.ds(first, last - first)],
                send_sem=ms_sem.at[e, p],
                recv_sem=mr_sem.at[e, p],
                device_id=(me_s, peer),
                device_id_type=MESH,
            )
            for p, peer in enumerate(net_peer)
        ]
        for copy in copies:
            copy.start()
        return copies

    def neighbours(e):
        if nets == 1:
            return [zero] * HB, [zero] * HB
        low = [jnp.where(has_left, msg_in[e, 0, HB + j], zero) for j in range(HB)]
        high = [jnp.where(has_right, msg_in[e, nets - 2, j], zero) for j in range(HB)]
        return low, high

    def total(e, partial):
        for p in range(nets - 1):
            partial = partial + msg_in[e, p, 2 * HB]
        return jnp.sum(partial, axis=1, keepdims=True)

    def wait(copies):
        for copy in copies:
            copy.wait()

    def transposed(e, w, partial):
        acc = [None] * (nb + 2 * HB)
        for i in edge:
            transpose_row(i, w[i], acc)
        copies = send(e, acc[:HB] + acc[HB + nb :], partial)
        for i in inner:
            transpose_row(i, w[i], acc)
        wait(copies)
        low, high = neighbours(e)
        z = acc[HB : HB + nb]
        for j in range(HB):
            z[j] = z[j] + low[j]
            z[nb - HB + j] = z[nb - HB + j] + high[j]
        return z

    def forward_with_halo(e, v, partial):
        copies = send(e, v[:HB] + v[nb - HB :], partial)
        for i in range(nb):
            hl[HB + i] = halves(v[i])
        w = [None] * nb
        for i in inner:
            w[i] = forward_row(i)
        wait(copies)
        low, high = neighbours(e)
        set_halo(low, high)
        for i in edge:
            w[i] = forward_row(i)
        return w

    def rows(ref):
        return [ref[i * R : (i + 1) * R, :] for i in range(nb)]

    def add_all(terms):
        while len(terms) > 1:
            terms = [
                terms[j] + terms[j + 1] if j + 1 < len(terms) else terms[j]
                for j in range(0, len(terms), 2)
            ]
        return terms[0]

    w = [bv[i * R : (i + 1) * R, :] - forward_row(i) for i in range(nb)]
    z = transposed(0, w, None)
    r0 = [z[i] - dv[i * R : (i + 1) * R, :] for i in range(nb)]
    part0 = add_all([v * v for v in r0])
    for i in range(nb):
        rv[i * R : (i + 1) * R, :] = r0[i]
    wa = forward_with_halo(1, r0, part0)
    norm0 = total(1, part0)
    for i in range(nb):
        w0[i * R : (i + 1) * R, :] = wa[i]
    pen = rows(penb)
    part_q = add_all(
        [p * v * v for p, v in zip(pen, rows(rv))] + [v * v for v in wa]
    )
    z = transposed(2, wa, part_q)
    a0 = norm0 / total(2, part_q)
    r0 = rows(rv)
    pen = rows(penb)
    r1 = [r0[i] - a0 * (pen[i] * r0[i] + z[i]) for i in range(nb)]
    part1 = add_all([v * v for v in r1])
    for i in range(nb):
        dv[i * R : (i + 1) * R, :] = r1[i]
        bv[i * R : (i + 1) * R, :] = xv[i * R : (i + 1) * R, :] + a0 * r0[i]
    wb = forward_with_halo(3, r1, part1)
    norm1 = total(3, part1)
    beta = norm1 / norm0
    d1 = [dv[i * R : (i + 1) * R, :] + beta * rv[i * R : (i + 1) * R, :] for i in range(nb)]
    ad = [wb[i] + beta * w0[i * R : (i + 1) * R, :] for i in range(nb)]
    part_q = add_all(
        [penb[i * R : (i + 1) * R, :] * d1[i] * d1[i] for i in range(nb)] + [v * v for v in ad]
    )
    wait(send(4, [], part_q))
    a1 = norm1 / total(4, part_q)
    for i in range(nb):
        rows_i = slice(i * R, (i + 1) * R)
        xv[rows_i, :] = jnp.maximum(bv[rows_i, :] + a1 * d1[i], 0.0)

    clipped = [xv[pl.ds(s, nb, stride=R), :] for s in range(L)]
    group = jnp.right_shift(jnp.int32(L * nodes), sec_rows[...])
    sums = clipped
    for b in range(L.bit_length() - 1):
        sums = [
            sums[s] + jnp.where(group > (1 << b), sums[s ^ (1 << b)], 0.0) for s in range(L)
        ]
    mine = sums[0]
    base = mine
    slot = 0
    for f, (at, masks) in enumerate(phases):
        sum_out[f] = mine
        copies = []
        for j, mask in enumerate(masks):
            copies.append(
                pltpu.make_async_remote_copy(
                    src_ref=sum_out.at[f],
                    dst_ref=sum_in.at[slot + j],
                    send_sem=ss_sem.at[slot + j],
                    recv_sem=sr_sem.at[slot + j],
                    device_id=(scen_peer(at, mask), me_n),
                    device_id_type=MESH,
                )
            )
        for copy in copies:
            copy.start()
        wait(copies)
        got = [sum_in[slot + j] for j in range(len(masks))]
        extra = jnp.where(group > (L << at), got[0], 0.0)
        if len(masks) == 3:
            extra = extra + jnp.where(group > (L << (at + 1)), got[1] + got[2], 0.0)
        mine = mine + extra
        slot += len(masks)
    shared = group >= L
    for s in range(L):
        sum_ref[s] = jnp.where(shared, mine, sums[s])
        clip_ref[s] = clipped[s]
    size_ref[...] = group.astype(jnp.float32)


def body(*args):
    x = args[0]
    mat = args[5]
    L, nb, blk = x.shape
    nnz = mat.shape[1]
    nets = lax.axis_size("net")
    nodes = lax.axis_size("scen")
    R = 2 * L
    others = max(nets - 1, 1)
    phases = phases_of(nodes)
    slots = max(sum(len(m) for _, m in phases), 1)
    f32 = jnp.float32
    V = pltpu.VMEM
    dma = pltpu.SemaphoreType.DMA
    scratch = [
        V((L, nb, blk), f32),
        V((L, nb, blk), f32),
        V((L, nb, blk), f32),
        V((nb, blk), f32),
        V((nb, blk), f32),
        V(mat.shape, f32),
        pltpu.SMEM((nnz, nb), jnp.int32),
        pltpu.SMEM((nb,), jnp.int32),
        V((nb, 2 * blk, nnz * blk), jnp.bfloat16),
        V((nb * R, blk), f32),
        V((nb * R, blk), f32),
        V((nb * R, blk), f32),
        V((nb * R, blk), f32),
        V((nb + 2 * HB, R, blk), f32),
        V((nb * R, blk), f32),
        V((nb * R, blk), f32),
        V((nb, blk), jnp.int32),
        V((others, L, nb, blk), f32),
        V((5, 2 * HB + 1, R, blk), f32),
        V((5, others, 2 * HB + 1, R, blk), f32),
        V((max(len(phases), 1), nb, blk), f32),
        V((slots, nb, blk), f32),
        dma((7,)),
        dma((nb,)),
        dma((others,)),
        dma((others,)),
        dma((5, others)),
        dma((5, others)),
        dma((slots,)),
        dma((slots,)),
    ]
    hbm_spec = pl.BlockSpec(memory_space=pltpu.HBM)
    vmem_spec = pl.BlockSpec(memory_space=pltpu.VMEM)
    sums, clipped, size = pl.pallas_call(
        functools.partial(kernel, nets, nodes),
        out_shape=(V(x.shape, f32), V(x.shape, f32), V((nb, blk), f32)),
        in_specs=[hbm_spec] * 8,
        out_specs=(vmem_spec, vmem_spec, vmem_spec),
        scratch_shapes=scratch,
        compiler_params=pltpu.CompilerParams(
            collective_id=0, has_side_effects=True, vmem_limit_bytes=60_000_000
        ),
    )(*args[:6], args[6].T, args[7])
    mean = sums / size[None]
    return mean, args[1] + args[4][None] * (clipped - mean)


def solution(mesh):
    placed = (
        P("scen", "net", None),
        P("scen", "net", None),
        P("scen", "net", None),
        P("net", None),
        P("net", None),
        P("net", None, None, None),
        P("net", None),
        P("net"),
    )
    fn = jax.shard_map(
        body,
        mesh=mesh,
        in_specs=placed,
        out_specs=(P("scen", "net", None), P("scen", "net", None)),
        check_vma=False,
    )
    return lambda *args: tuple(fn(*args))
```
